32 devices in a mesh: grp: 2 (over y), lon: 4 (over z), lat: 2 (over x), lvl: 2 (over core).
Axes of the slice: x: 2, y: 2, z: 4, core: 2. Of those that a mesh axis runs over, the one named last changes fastest.
Arguments:
- tokens: bfloat16 [4, 24, 96, 512], P(('grp', 'lvl'), 'lat', 'lon'), parts along dimension 0, may hold values from -8 to 8
- fine_tags: int32 [4, 24, 96], P(('grp', 'lvl'), 'lat', 'lon'), parts along dimension 0, may hold values from 1 to 3
- coarse_tags: int32 [4, 12, 48], P(('grp', 'lvl'), 'lat', 'lon'), parts along dimension 0, may hold values from 1 to 3
- fine_gain: float32 [512], replicated, may hold values from 0.25 to 1.75
- fine_inward: bfloat16 [3, 512, 512], P(None, 'lon', 'lvl'), may hold values from -0.25 to 0.25
- fine_outward: bfloat16 [512, 512], P('lon', 'lvl'), may hold values from -0.25 to 0.25
- fine_table: float32 [16, 253], replicated, may hold values from -2 to 300
- merge_gain: float32 [2048], replicated, may hold values from 0.25 to 1.75
- merge_weight: bfloat16 [1024, 2048], P('lon', 'lvl'), may hold values from -0.125 to 0.125
- coarse_gain: float32 [1024], replicated, may hold values from 0.25 to 1.75
- coarse_inward: bfloat16 [3, 1024, 1024], P(None, 'lon', 'lvl'), may hold values from -0.1875 to 0.1875
- coarse_outward: bfloat16 [1024, 1024], P('lon', 'lvl'), may hold values from -0.1875 to 0.1875
- coarse_table: float32 [32, 253], replicated, may hold values from -2 to 300
Outputs:
- fine_out: bfloat16 [4, 24, 96, 512], P(('grp', 'lvl'), 'lat', 'lon'), parts along dimension 0
- coarse_out: bfloat16 [4, 12, 48, 1024], P(('grp', 'lvl'), 'lat', 'lon'), parts along dimension 0
The draws below stay inside these ranges and needn't reach their ends.
There are 2 independent parts, one for each index of `grp`. The reference program is written for one: setup_inputs(seed, part) draws one part's arguments, and reference() takes and returns one part's arrays. A program takes and returns all parts, laid end to end along the dimension named above; an argument that names none is the same for every part. Nothing has to cross between parts.
All inputs are finite; a program needn't handle non-finite values.
Results may differ from the reference program's by a relative error of at most 0.017.
Values may be sent and summed in bfloat16 or wider, within the bound.
No kernel may reach another device: no remote copies, remote signals or barrier semaphores. Data moves between devices by JAX's collectives and lax.ppermute only.
A program may use at most 64 MiB of HBM per device.

```python
import jax
import jax.numpy as jnp
from jax import lax

D1 = 512
HEADS1 = 16
D2 = 1024
HEADS2 = 32
WIN_LAT = 6
WIN_LON = 12
LEVELS = 2
LATS = 24
LONS = 96


def draw_tokens(key, part):
    normal_key = jax.random.fold_in(key, 0)
    sample = jax.random.normal(normal_key, (LEVELS, LATS, LONS, D1), jnp.float32)
    return jnp.clip(sample, -8.0, 8.0).astype(jnp.float32).astype(jnp.bfloat16)


def table_draw(seed_key, head_count):
    base_key = jax.random.fold_in(seed_key, 0)
    span_lat = 2 * WIN_LAT - 1
    span_lon = 2 * WIN_LON - 1
    baseline = jax.random.uniform(base_key, (head_count, span_lat * span_lon), jnp.float32, -2.0, 2.0)
    return baseline


def draw_fine_table(key, part):
    return table_draw(jax.random.fold_in(key, 11), HEADS1)


def draw_coarse_table(key, part):
    return table_draw(jax.random.fold_in(key, 23), HEADS2)


def with_ends(entries, stream_key, smallest, high):
    longest = entries.shape.index(max(entries.shape))
    spots = []
    for shift in (0, 1):
        where = [jax.random.randint(jax.random.fold_in(stream_key, axis), (), 0, length) for axis, length in enumerate(entries.shape)]
        where[longest] = (where[longest] + shift) % entries.shape[longest]
        spots.append(tuple(where))
    return entries.at[spots[0]].set(smallest).at[spots[1]].set(high)


def level_of(own_key, extent, pieces, least, largest):
    factor_of, own = 1.0, jax.random.fold_in(own_key, 6)
    for position, blocks in pieces:
        steps = jnp.exp(jax.random.uniform(jax.random.fold_in(own, position), (blocks,), jnp.float32, least / len(pieces), largest / len(pieces)))
        factor_of = factor_of * jnp.repeat(steps, extent[position] // blocks).reshape([-1 if axis == position else 1 for axis in range(len(extent))])
    return factor_of


def gaussian(own_key, dims, width, limit, cuts=(), kind=jnp.bfloat16):
    array = width * jax.random.normal(own_key, dims, jnp.float32)
    if cuts:
        array = array * level_of(own_key, dims, cuts, -0.22, 0.18)
    return jnp.clip(array, -limit, limit).astype(kind)


def setup_inputs(seed: int = 0, part: int = 0) -> dict:
    splits = jax.random.split(jax.random.key(seed), 14)
    part_keys = jax.random.split(jax.random.fold_in(splits[13], part), 14)
    tokens = draw_tokens(jax.random.fold_in(jax.random.fold_in(splits[13], part), 71), part)
    fine_tags = with_ends(jax.random.randint(part_keys[1], (LEVELS, LATS, LONS), 1, 4), jax.random.fold_in(part_keys[1], 1), 1, 3).astype(jnp.int32)
    coarse_tags = with_ends(jax.random.randint(part_keys[2], (LEVELS, LATS // 2, LONS // 2), 1, 4), jax.random.fold_in(part_keys[2], 1), 1, 3).astype(jnp.int32)
    fine_gain = jnp.clip(1.0 + 0.15 * jax.random.normal(splits[3], (D1,), jnp.float32), 0.25, 1.75)
    fine_inward = gaussian(splits[4], (3, D1, D1), D1 ** -0.5, 0.25, ((1, 4), (2, 2)))
    fine_outward = gaussian(splits[5], (D1, D1), D1 ** -0.5, 0.25, ((0, 4), (1, 2)))
    fine_table = draw_fine_table(jax.random.fold_in(splits[13], 71), part)
    merge_gain = jnp.clip(1.0 + 0.15 * jax.random.normal(splits[7], (4 * D1,), jnp.float32), 0.25, 1.75)
    merge_weight = gaussian(splits[8], (D2, 4 * D1), (4 * D1) ** -0.5, 0.125, ((0, 4), (1, 2)))
    coarse_gain = jnp.clip(1.0 + 0.15 * jax.random.normal(splits[9], (D2,), jnp.float32), 0.25, 1.75)
    coarse_inward = gaussian(splits[10], (3, D2, D2), D2 ** -0.5, 0.1875, ((1, 4), (2, 2)))
    coarse_outward = gaussian(splits[11], (D2, D2), D2 ** -0.5, 0.1875, ((0, 4), (1, 2)))
    coarse_table = draw_coarse_table(jax.random.fold_in(splits[13], 71), part)
    return dict(tokens=tokens, fine_tags=fine_tags, coarse_tags=coarse_tags, fine_gain=fine_gain, fine_inward=fine_inward, fine_outward=fine_outward, fine_table=fine_table, merge_gain=merge_gain, merge_weight=merge_weight, coarse_gain=coarse_gain, coarse_inward=coarse_inward, coarse_outward=coarse_outward, coarse_table=coarse_table)


EPSILON = 1e-05

def layer_norm(values, scales):
    widened = values.astype(jnp.float32)
    center = widened - lax.optimization_barrier(jnp.mean(widened, axis=-1, keepdims=True))
    spread = lax.optimization_barrier(jnp.mean(center * center, axis=-1, keepdims=True))
    return center * lax.rsqrt(spread + EPSILON) * scales.astype(jnp.float32)

def bias_blocks(bias_table, win_lat, win_lon):
    head_count = bias_table.shape[0]
    span_lat = 2 * win_lat - 1
    span_lon = 2 * win_lon - 1
    table_grid = bias_table.astype(jnp.float32).reshape(head_count, span_lat, span_lon)
    lat_pos = jnp.arange(win_lat)
    lon_pos = jnp.arange(win_lon)
    lat_onehot = (lat_pos[:, None, None] - lat_pos[None, :, None] + win_lat - 1 == jnp.arange(span_lat)[None, None, :]).astype(jnp.float32)
    lon_onehot = (lon_pos[:, None, None] - lon_pos[None, :, None] + win_lon - 1 == jnp.arange(span_lon)[None, None, :]).astype(jnp.float32)
    along_lon = jnp.einsum('hab,ijb->haij', table_grid, lon_onehot, precision=lax.Precision.HIGHEST)
    blocks = jnp.einsum('kla,haij->hkilj', lat_onehot, along_lon, precision=lax.Precision.HIGHEST)
    return blocks.reshape(head_count, win_lat * win_lon, win_lat * win_lon)

def split_windows(array_in, win_lat, win_lon):
    levels, lat_len, lon_len = array_in.shape[:3]
    trailing = array_in.shape[3:]
    blocked = array_in.reshape((levels, lat_len // win_lat, win_lat, lon_len // win_lon, win_lon) + trailing)
    blocked = jnp.moveaxis(blocked, 3, 2)
    return blocked.reshape((levels, lat_len // win_lat, lon_len // win_lon, win_lat * win_lon) + trailing)

def join_windows(array_in, win_lat, win_lon):
    levels, lat_bands, lon_bands = array_in.shape[:3]
    trailing = array_in.shape[4:]
    blocked = array_in.reshape((levels, lat_bands, lon_bands, win_lat, win_lon) + trailing)
    blocked = jnp.moveaxis(blocked, 3, 2)
    return blocked.reshape((levels, lat_bands * win_lat, lon_bands * win_lon) + trailing)

def attend(query_grid, key_grid, value_grid, tag_grid, bias_table, win_lat, win_lon):
    head_count = bias_table.shape[0]
    features = query_grid.shape[-1]
    head_size = features // head_count
    offsets_bias = bias_blocks(bias_table, win_lat, win_lon)

    def heads_of(array_in):
        blocks = split_windows(array_in, win_lat, win_lon)
        return blocks.reshape((-1,) + blocks.shape[2:4] + (head_count, head_size)).astype(jnp.float32)
    query_heads = heads_of(query_grid)
    key_heads = heads_of(key_grid)
    value_heads = heads_of(value_grid)
    tag_blocks = split_windows(tag_grid, win_lat, win_lon)
    tag_blocks = tag_blocks.reshape((-1,) + tag_blocks.shape[2:4])

    def one_band(inputs):
        query_band, key_band, value_band, tag_band = inputs
        scores = jnp.einsum('bphd,bqhd->bhpq', query_band, key_band, precision=lax.Precision.HIGHEST)
        scores = scores * head_size ** (-0.5) + offsets_bias
        allowed = tag_band[:, None, :, None] == tag_band[:, None, None, :]
        scores = jnp.where(allowed, scores, -jnp.inf)
        highest = lax.optimization_barrier(jnp.max(scores, axis=-1, keepdims=True))
        weights = jnp.exp(scores - highest)
        shares = (weights / lax.optimization_barrier(jnp.sum(weights, axis=-1, keepdims=True))).astype(jnp.bfloat16)
        blended = jnp.einsum('bhpq,bqhd->bphd', shares.astype(jnp.float32), value_band, precision=lax.Precision.HIGHEST)
        return blended.astype(jnp.bfloat16).reshape(blended.shape[:2] + (features,))
    blended = lax.map(one_band, (query_heads, key_heads, value_heads, tag_blocks))
    levels, lat_len = query_grid.shape[:2]
    blended = blended.reshape((levels, lat_len // win_lat) + blended.shape[1:])
    return join_windows(blended, win_lat, win_lon)

def window_block(stream, tag_grid, gain_row, inward, outward, bias_table):
    levels, lat_len, lon_len, features = stream.shape
    normed = layer_norm(stream, gain_row).astype(jnp.bfloat16)
    flattened = normed.reshape(-1, features)
    lat_half = WIN_LAT // 2
    lon_half = WIN_LON // 2

    def arrange(array_in):
        rolled = jnp.roll(array_in, -lon_half, axis=2)
        padding = [(0, 0), (lat_half, lat_half)] + [(0, 0)] * (array_in.ndim - 2)
        return jnp.pad(rolled, padding)
    projected = []
    for member in range(3):
        product = jnp.dot(flattened, inward[member], preferred_element_type=jnp.float32).astype(jnp.bfloat16)
        projected.append(arrange(product.reshape(levels, lat_len, lon_len, features)))
    blended = attend(projected[0], projected[1], projected[2], arrange(tag_grid), bias_table, WIN_LAT, WIN_LON)
    blended = jnp.roll(blended[:, lat_half:lat_half + lat_len], lon_half, axis=2)
    update = jnp.dot(blended.reshape(-1, features), outward.T, preferred_element_type=jnp.float32)
    return (stream.astype(jnp.float32) + update.reshape(stream.shape)).astype(jnp.bfloat16)

def group_patches(stream):
    levels, lat_len, lon_len, features = stream.shape
    blocked = stream.reshape(levels, lat_len // 2, 2, lon_len // 2, 2, features)
    blocked = jnp.moveaxis(blocked, 3, 2)
    return blocked.reshape(levels, lat_len // 2, lon_len // 2, 4 * features)

def reference(tokens, fine_tags, coarse_tags, fine_gain, fine_inward, fine_outward, fine_table, merge_gain, merge_weight, coarse_gain, coarse_inward, coarse_outward, coarse_table):
    fine_result = window_block(tokens, fine_tags, fine_gain, fine_inward, fine_outward, fine_table)
    grouped = group_patches(fine_result)
    merged_normed = layer_norm(grouped, merge_gain).astype(jnp.bfloat16)
    levels, lat_len, lon_len, wide_features = merged_normed.shape
    coarse_in = jnp.dot(merged_normed.reshape(-1, wide_features), merge_weight.T, preferred_element_type=jnp.float32)
    coarse_in = coarse_in.astype(jnp.bfloat16).reshape(levels, lat_len, lon_len, -1)
    coarse_result = window_block(coarse_in, coarse_tags, coarse_gain, coarse_inward, coarse_outward, coarse_table)
    return (fine_result, coarse_result)
```

```python
import functools

import jax
import jax.numpy as jnp
from jax import lax
from jax.experimental import pallas as pl
from jax.experimental.pallas import tpu as pltpu
from jax.sharding import PartitionSpec as P

WIN_LAT = 6
WIN_LON = 12
HALF_LAT = WIN_LAT // 2
HALF_LON = WIN_LON // 2
WIN = WIN_LAT * WIN_LON
HEAD = 32
LANES = 128
PER_GROUP = LANES // HEAD
SPAN_LON = 2 * WIN_LON - 1
SPAN_LAT = 2 * WIN_LAT - 1
EPSILON = 1e-05
VMEM = pl.BlockSpec(memory_space=pltpu.VMEM)
PARAMS = pltpu.CompilerParams(vmem_limit_bytes=56 * 1024 * 1024)


def shifts(count, step):
    return [(i, (i + step) % count) for i in range(count)]


def norm_rows(values, scales):
    center = values - jnp.mean(values, axis=-1, keepdims=True)
    spread = jnp.mean(center * center, axis=-1, keepdims=True)
    return center * lax.rsqrt(spread + EPSILON) * scales


def block_kernel(
    x_ref, col_ref, row_ref, gain_ref, in_ref, out_w_ref, bias_ref, out_ref,
    q_s, k_s, v_s, mask_s, mix_s,
):
    windows, _, features = x_ref.shape
    groups = features // LANES
    rows = windows * WIN
    stream = x_ref[...].astype(jnp.float32).reshape(rows, features)
    normed = norm_rows(stream, gain_ref[...]).astype(jnp.bfloat16)
    for member, dest in enumerate((q_s, k_s, v_s)):
        product = jnp.dot(normed, in_ref[member], preferred_element_type=jnp.float32)
        for w in range(windows):
            for g in range(groups):
                block = product[w * WIN : (w + 1) * WIN, g * LANES : (g + 1) * LANES]
                dest[w * groups + g] = block.astype(jnp.bfloat16)
    for w in range(windows):
        mask_s[w] = jnp.where(col_ref[w] == row_ref[w], 0.0, -jnp.inf)
    lane_head = lax.broadcasted_iota(jnp.int32, (1, LANES), 1) // HEAD

    def one_group(step, carry):
        w = step // groups
        g = step % groups
        query = q_s[step]
        key = k_s[step]
        value = v_s[step]
        mask = mask_s[w]
        total = jnp.zeros((WIN, LANES), jnp.float32)
        for h in range(PER_GROUP):
            own = lane_head == h
            picked = jnp.where(own, query, jnp.zeros_like(query))
            scores = lax.dot_general(
                picked, key, (((1,), (1,)), ((), ())), preferred_element_type=jnp.float32
            )
            scores = scores * HEAD ** (-0.5) + bias_ref[g * PER_GROUP + h] + mask
            weights = jnp.exp(scores - jnp.max(scores, axis=-1, keepdims=True))
            shares = weights / jnp.sum(weights, axis=-1, keepdims=True)
            chosen = jnp.where(own, value, jnp.zeros_like(value))
            total = total + jnp.dot(
                shares.astype(jnp.bfloat16), chosen, preferred_element_type=jnp.float32
            )
        mix_s[step] = total
        return carry

    lax.fori_loop(0, windows * groups, one_group, 0)
    mixed = jnp.concatenate(
        [
            jnp.concatenate([mix_s[w * groups + g] for w in range(windows)], axis=0)
            for g in range(groups)
        ],
        axis=1,
    ).astype(jnp.bfloat16)
    update = lax.dot_general(
        mixed, out_w_ref[...], (((1,), (1,)), ((), ())), preferred_element_type=jnp.float32
    )
    summed = x_ref[...].astype(jnp.float32).reshape(rows, features) + update
    out_ref[...] = summed.astype(jnp.bfloat16).reshape(windows, WIN, features)


def window_block(stream, tags, gain, inward, outward, bias):
    windows, _, features = stream.shape
    groups = features // LANES
    steps = windows * groups
    return pl.pallas_call(
        block_kernel,
        out_shape=jax.ShapeDtypeStruct(stream.shape, jnp.bfloat16),
        in_specs=[VMEM] * 7,
        out_specs=VMEM,
        scratch_shapes=[
            pltpu.VMEM((steps, WIN, LANES), jnp.bfloat16),
            pltpu.VMEM((steps, WIN, LANES), jnp.bfloat16),
            pltpu.VMEM((steps, WIN, LANES), jnp.bfloat16),
            pltpu.VMEM((windows, WIN, WIN), jnp.float32),
            pltpu.VMEM((steps, WIN, LANES), jnp.float32),
        ],
        compiler_params=PARAMS,
        cost_estimate=pl.CostEstimate(
            flops=8 * windows * WIN * features * features,
            transcendentals=0,
            bytes_accessed=8 * features * features,
        ),
    )(stream, tags[:, :, None], tags[:, None, :], gain.reshape(1, -1), inward, outward, bias)


def merge_kernel(x_ref, gain_ref, w_ref, out_ref):
    normed = norm_rows(x_ref[...].astype(jnp.float32), gain_ref[...]).astype(jnp.bfloat16)
    out_ref[...] = lax.dot_general(
        normed, w_ref[...], (((1,), (1,)), ((), ())), preferred_element_type=jnp.float32
    ).astype(jnp.bfloat16)


def merge(grouped, gain, weight):
    return pl.pallas_call(
        merge_kernel,
        out_shape=jax.ShapeDtypeStruct((grouped.shape[0], weight.shape[0]), jnp.bfloat16),
        in_specs=[VMEM] * 3,
        out_specs=VMEM,
        compiler_params=PARAMS,
        cost_estimate=pl.CostEstimate(
            flops=2 * grouped.shape[0] * weight.size,
            transcendentals=0,
            bytes_accessed=2 * weight.size,
        ),
    )(grouped, gain.reshape(1, -1), weight)


BAND = 256


def bias_kernel(*refs):
    count = len(refs) // 2
    for src, dest in zip(refs[:count], refs[count:]):

        def one_head(h, carry, src=src, dest=dest):
            strip = src[h]
            for r in range(WIN_LAT):
                start = WIN_LON * (WIN_LAT - 1 - r)
                moved = strip if start == 0 else pltpu.roll(strip, BAND - start, 1)
                dest[h, WIN_LON * r : WIN_LON * (r + 1), :] = moved[:WIN_LON, :WIN]
            return carry

        lax.fori_loop(0, src.shape[0], one_head, 0)


def table_strips(table):
    entry = jnp.arange(SPAN_LAT * SPAN_LON)[:, None, None]
    lon_i = jnp.arange(WIN_LON)[None, :, None]
    lane = jnp.arange(BAND)[None, None, :]
    wanted = (SPAN_LAT - 1 - lane // WIN_LON) * SPAN_LON + lon_i - lane % WIN_LON + WIN_LON - 1
    onehot = ((entry == wanted) & (lane < SPAN_LAT * WIN_LON)).astype(jnp.float32)
    strips = jnp.dot(table, onehot.reshape(entry.shape[0], -1), precision=lax.Precision.HIGHEST)
    return strips.reshape(table.shape[0], WIN_LON, BAND)


def all_bias(*tables):
    strips = [table_strips(table) for table in tables]
    return pl.pallas_call(
        bias_kernel,
        out_shape=[jax.ShapeDtypeStruct((t.shape[0], WIN, WIN), jnp.float32) for t in tables],
        in_specs=[VMEM] * len(tables),
        out_specs=[VMEM] * len(tables),
        compiler_params=PARAMS,
    )(*strips)


def both(step):
    def send(array):
        lats, lons = lax.axis_size("lat"), lax.axis_size("lon")
        pairs = [
            (i * lats + a, (i + step) % lons * lats + (a + step) % lats)
            for i in range(lons)
            for a in range(lats)
        ]
        return lax.ppermute(array, ("lon", "lat"), pairs)

    return send


def along(axis, step):
    return lambda array: lax.ppermute(array, axis, shifts(lax.axis_size(axis), step))


def forward(grid):
    right = along("lon", -1)(grid[HALF_LAT:, :HALF_LON])
    below = along("lat", -1)(grid[:HALF_LAT, HALF_LON:])
    corner = both(-1)(grid[:HALF_LAT, :HALF_LON])
    upper = jnp.concatenate([grid[HALF_LAT:, HALF_LON:], right], axis=1)
    lower = jnp.concatenate([below, corner], axis=1)
    return jnp.concatenate([upper, lower], axis=0)


def backward(grid):
    left = along("lon", 1)(grid[:-HALF_LAT, -HALF_LON:])
    above = along("lat", 1)(grid[-HALF_LAT:, :-HALF_LON])
    corner = both(1)(grid[-HALF_LAT:, -HALF_LON:])
    upper = jnp.concatenate([corner, above], axis=1)
    lower = jnp.concatenate([left, grid[:-HALF_LAT, :-HALF_LON]], axis=1)
    return jnp.concatenate([upper, lower], axis=0)


def split_windows(grid):
    lats, lons = grid.shape[:2]
    blocked = grid.reshape((lats // WIN_LAT, WIN_LAT, lons // WIN_LON, WIN_LON) + grid.shape[2:])
    return jnp.moveaxis(blocked, 2, 1).reshape((-1, WIN) + grid.shape[2:])


def join_windows(windows, lats, lons):
    blocked = windows.reshape(
        (lats // WIN_LAT, lons // WIN_LON, WIN_LAT, WIN_LON) + windows.shape[2:]
    )
    return jnp.moveaxis(blocked, 2, 1).reshape((lats, lons) + windows.shape[2:])


def shifted_tags(tags):
    moved = forward(tags)
    rows = jnp.arange(moved.shape[0])[:, None]
    last = lax.axis_index("lat") == lax.axis_size("lat") - 1
    past = jnp.logical_and(last, rows >= moved.shape[0] - HALF_LAT)
    return split_windows(jnp.where(past, moved + 4, moved)).astype(jnp.float32)


def group_patches(grid):
    lats, lons, features = grid.shape
    blocked = grid.reshape(lats // 2, 2, lons // 2, 2, features)
    return jnp.moveaxis(blocked, 2, 1).reshape(-1, 4 * features)


def full(weight, dim):
    return lax.all_gather(
        lax.all_gather(weight, "lvl", axis=dim + 1, tiled=True), "lon", axis=dim, tiled=True
    )


def shards(
    tokens,
    fine_tags,
    coarse_tags,
    fine_gain,
    fine_inward,
    fine_outward,
    fine_table,
    merge_gain,
    merge_weight,
    coarse_gain,
    coarse_inward,
    coarse_outward,
    coarse_table,
):
    lats, lons = tokens.shape[1:3]
    fine_bias, coarse_bias = all_bias(fine_table, coarse_table)
    fine_marks = shifted_tags(fine_tags[0])
    coarse_marks = shifted_tags(coarse_tags[0])
    stream = split_windows(forward(tokens[0]))
    fine = window_block(
        stream, fine_marks, fine_gain, full(fine_inward, 1), full(fine_outward, 0), fine_bias
    )
    fine_grid = join_windows(fine, lats, lons)
    grouped = group_patches(forward(fine_grid))
    coarse_in = merge(grouped, merge_gain, full(merge_weight, 0))
    coarse = window_block(
        coarse_in.reshape((-1, WIN) + coarse_in.shape[1:]),
        coarse_marks,
        coarse_gain,
        full(coarse_inward, 1),
        full(coarse_outward, 0),
        coarse_bias,
    )
    coarse_grid = join_windows(coarse, lats // 2, lons // 2)
    return backward(fine_grid)[None], backward(coarse_grid)[None]


def solution(mesh):
    placed = (
        P(("grp", "lvl"), "lat", "lon", None),
        P(("grp", "lvl"), "lat", "lon"),
        P(("grp", "lvl"), "lat", "lon"),
        P(),
        P(None, "lon", "lvl"),
        P("lon", "lvl"),
        P(),
        P(),
        P("lon", "lvl"),
        P(),
        P(None, "lon", "lvl"),
        P("lon", "lvl"),
        P(),
    )
    return jax.shard_map(
        shards,
        mesh=mesh,
        in_specs=placed,
        out_specs=(P(("grp", "lvl"), "lat", "lon", None), P(("grp", "lvl"), "lat", "lon", None)),
        check_vma=False,
    )
```

```python
import functools

import jax
import jax.numpy as jnp
from jax import lax
from jax.experimental import pallas as pl
from jax.experimental.pallas import tpu as pltpu
from jax.sharding import PartitionSpec as P

WIN_LAT = 6
WIN_LON = 12
HALF_LAT = WIN_LAT // 2
HALF_LON = WIN_LON // 2
WIN = WIN_LAT * WIN_LON
HEAD = 32
LANES = 128
PER_GROUP = LANES // HEAD
SPAN_LON = 2 * WIN_LON - 1
SPAN_LAT = 2 * WIN_LAT - 1
EPSILON = 1e-05
VMEM = pl.BlockSpec(memory_space=pltpu.VMEM)
ANY = pl.BlockSpec(memory_space=pl.ANY)
PARAMS = pltpu.CompilerParams(vmem_limit_bytes=56 * 1024 * 1024)
FINE_TAG = 0
COARSE_TAG = 1


def shifts(count, step):
    return [(i, (i + step) % count) for i in range(count)]


def norm_rows(values, scales):
    center = values - jnp.mean(values, axis=-1, keepdims=True)
    spread = jnp.mean(center * center, axis=-1, keepdims=True)
    return center * lax.rsqrt(spread + EPSILON) * scales


def gather(shard):
    lons, grps, lats = (lax.axis_size(axis) for axis in ("lon", "grp", "lat"))
    rows = shard.shape[0]
    piece = rows // (grps * lats)
    if lons == 1 or rows % (16 * grps * lats):
        pieces = [(lax.all_gather(shard, "lon", axis=0, tiled=True), None)]
    else:
        part = lax.axis_index("grp") * lats + lax.axis_index("lat")
        mine = lax.dynamic_slice_in_dim(shard, part * piece, piece, 0)
        got = jnp.stack([along("lon", step)(mine) for step in range(1, lons)])
        pieces = [(shard, "own"), (got, (0, 0))]
        for g in range(grps):
            for a in range(lats):
                if (g, a) != (0, 0):
                    pieces.append((across("grp", "lat", g, a)(got), (g, a)))
    lvls = lax.axis_size("lvl")
    arrays, places = [], []
    for step in range(lvls):
        for array, place in pieces:
            arrays.append(along("lvl", step)(array) if step else array)
            places.append((step, place))
    return arrays, tuple(places)


def copies(refs, places, dest, sems):
    lons, grps, lats, lvls = (lax.axis_size(axis) for axis in ("lon", "grp", "lat", "lvl"))
    lon, grp, lat, lvl = (lax.axis_index(axis) for axis in ("lon", "grp", "lat", "lvl"))
    rows = dest.shape[1] // lons
    result = []
    for ref, (step, place) in zip(refs, places):
        half = lax.rem(lvl - step + lvls, lvls)
        if place is None:
            blocks = [(ref, 0)]
        elif place == "own":
            blocks = [(ref, lon * rows)]
        else:
            piece = ref.shape[1]
            part = lax.rem(grp - place[0] + grps, grps) * lats + lax.rem(lat - place[1] + lats, lats)
            blocks = [
                (ref.at[k - 1], lax.rem(lon - k + lons, lons) * rows + part * piece)
                for k in range(1, lons)
            ]
        for source, start in blocks:
            size = source.shape[0]
            target = dest.at[half, pl.ds(pl.multiple_of(start, 16), size)]
            result.append(pltpu.make_async_copy(source, target, sems.at[len(result)]))
    return result


def copy_count(places, lons):
    return sum(1 if place in (None, "own") else lons - 1 for _, place in places)


def block_kernel(places, features, tag_lane, per_band, *refs):
    pieces = len(places)
    x_ref, gain_ref, bias_ref = refs[:3]
    parts = refs[3 : 3 + pieces]
    out_ref, w_s, sems, q_s, k_s, v_s, mask_s, mix_s = refs[3 + pieces :]
    loads = copies(parts, places, w_s, sems)
    for load in loads:
        load.start()
    windows = x_ref.shape[0]
    groups = features // LANES
    rows = windows * WIN
    lvls = w_s.shape[0]
    width = features // lvls
    stream = x_ref[:, :, :features].astype(jnp.float32).reshape(rows, features)
    normed = norm_rows(stream, gain_ref[...]).astype(jnp.bfloat16)
    last = lax.axis_index("lat") == lax.axis_size("lat") - 1
    place = lax.broadcasted_iota(jnp.int32, (WIN, LANES), 0)
    for w in range(windows):
        extra = x_ref[w, :, features:].astype(jnp.float32)
        if w >= windows - per_band:
            past = jnp.logical_and(last, place >= WIN // 2)
            extra = extra + jnp.where(past, 4.0, 0.0)
        turned = jnp.transpose(extra)
        mask_s[w] = jnp.where(
            extra[:, tag_lane : tag_lane + 1] == turned[tag_lane : tag_lane + 1, :], 0.0, -jnp.inf
        )
    for load in loads:
        load.wait()
    for half in range(lvls):
        product = jnp.dot(normed, w_s[half, :, : 3 * width], preferred_element_type=jnp.float32)
        for member, dest in enumerate((q_s, k_s, v_s)):
            for w in range(windows):
                for g in range(width // LANES):
                    start = member * width + g * LANES
                    block = product[w * WIN : (w + 1) * WIN, start : start + LANES]
                    dest[w * groups + half * (width // LANES) + g] = block.astype(jnp.bfloat16)
    lane_head = lax.broadcasted_iota(jnp.int32, (1, LANES), 1) // HEAD

    def one_group(step, carry):
        w = step // groups
        g = step % groups
        query = q_s[step]
        key = k_s[step]
        value = v_s[step]
        mask = mask_s[w]
        total = jnp.zeros((WIN, LANES), jnp.float32)
        for h in range(PER_GROUP):
            own = lane_head == h
            picked = jnp.where(own, query, jnp.zeros_like(query))
            scores = lax.dot_general(
                picked, key, (((1,), (1,)), ((), ())), preferred_element_type=jnp.float32
            )
            scores = scores * HEAD ** (-0.5) + bias_ref[g * PER_GROUP + h] + mask
            weights = jnp.exp(scores - jnp.max(scores, axis=-1, keepdims=True))
            shares = weights / jnp.sum(weights, axis=-1, keepdims=True)
            chosen = jnp.where(own, value, jnp.zeros_like(value))
            total = total + jnp.dot(
                shares.astype(jnp.bfloat16), chosen, preferred_element_type=jnp.float32
            )
        mix_s[step] = total
        return carry

    lax.fori_loop(0, windows * groups, one_group, 0)
    total = x_ref[:, :, :features].astype(jnp.float32).reshape(rows, features)
    for half in range(lvls):
        mixed = jnp.concatenate(
            [
                jnp.concatenate([mix_s[w * groups + g] for w in range(windows)], axis=0)
                for g in range(half * (width // LANES), (half + 1) * (width // LANES))
            ],
            axis=1,
        ).astype(jnp.bfloat16)
        total = total + lax.dot_general(
            mixed,
            w_s[half, :, 3 * width :],
            (((1,), (1,)), ((), ())),
            preferred_element_type=jnp.float32,
        )
    out_ref[:, :, :features] = total.astype(jnp.bfloat16).reshape(windows, WIN, features)
    out_ref[:, :, features:] = x_ref[:, :, features:]


def window_block(stream, per_band, features, tag_lane, gain, weight, bias):
    arrays, places = weight
    windows = stream.shape[0]
    groups = features // LANES
    steps = windows * groups
    lons, lvls = lax.axis_size("lon"), lax.axis_size("lvl")
    return pl.pallas_call(
        functools.partial(block_kernel, places, features, tag_lane, per_band),
        out_shape=jax.ShapeDtypeStruct(stream.shape, jnp.bfloat16),
        in_specs=[VMEM] * 3 + [ANY] * len(arrays),
        out_specs=VMEM,
        scratch_shapes=[
            pltpu.VMEM((lvls, features, 4 * features // lvls), jnp.bfloat16),
            pltpu.SemaphoreType.DMA((copy_count(places, lons),)),
            pltpu.VMEM((steps, WIN, LANES), jnp.bfloat16),
            pltpu.VMEM((steps, WIN, LANES), jnp.bfloat16),
            pltpu.VMEM((steps, WIN, LANES), jnp.bfloat16),
            pltpu.VMEM((windows, WIN, WIN), jnp.float32),
            pltpu.VMEM((steps, WIN, LANES), jnp.float32),
        ],
        compiler_params=PARAMS,
        cost_estimate=pl.CostEstimate(
            flops=8 * windows * WIN * features * features,
            transcendentals=0,
            bytes_accessed=8 * features * features,
        ),
    )(stream, gain.reshape(1, -1), bias, *arrays)


def merge_kernel(places, features, *refs):
    pieces = len(places)
    x_ref, gain_ref = refs[:2]
    parts = refs[2 : 2 + pieces]
    out_ref, w_s, sems = refs[2 + pieces :]
    loads = copies(parts, places, w_s, sems)
    for load in loads:
        load.start()
    stride = x_ref.shape[1] // 4
    blocks = [x_ref[:, k * stride : k * stride + features] for k in range(4)]
    stream = jnp.concatenate(blocks, axis=1).astype(jnp.float32)
    normed = norm_rows(stream, gain_ref[...]).astype(jnp.bfloat16)
    lvls, outs, width = w_s.shape
    for load in loads:
        load.wait()
    total = jnp.zeros((x_ref.shape[0], outs), jnp.float32)
    for half in range(lvls):
        total = total + lax.dot_general(
            normed[:, half * width : (half + 1) * width],
            w_s[half],
            (((1,), (1,)), ((), ())),
            preferred_element_type=jnp.float32,
        )
    out_ref[:, :outs] = total.astype(jnp.bfloat16)
    out_ref[:, outs:] = x_ref[:, features:stride]


def merge(grouped, features, gain, weight):
    arrays, places = weight
    lons, lvls = lax.axis_size("lon"), lax.axis_size("lvl")
    width = 4 * features // lvls
    return pl.pallas_call(
        functools.partial(merge_kernel, places, features),
        out_shape=jax.ShapeDtypeStruct((grouped.shape[0], 2 * features + LANES), jnp.bfloat16),
        in_specs=[VMEM] * 2 + [ANY] * len(arrays),
        out_specs=VMEM,
        scratch_shapes=[
            pltpu.VMEM((lvls, 2 * features, width), jnp.bfloat16),
            pltpu.SemaphoreType.DMA((copy_count(places, lons),)),
        ],
        compiler_params=PARAMS,
        cost_estimate=pl.CostEstimate(
            flops=16 * grouped.shape[0] * features * features,
            transcendentals=0,
            bytes_accessed=16 * features * features,
        ),
    )(grouped, gain.reshape(1, -1), *arrays)


BAND = 256


def bias_kernel(*refs):
    count = len(refs) // 2
    for src, dest in zip(refs[:count], refs[count:]):

        def one_head(h, carry, src=src, dest=dest):
            strip = src[h]
            for r in range(WIN_LAT):
                start = WIN_LON * (WIN_LAT - 1 - r)
                moved = strip if start == 0 else pltpu.roll(strip, BAND - start, 1)
                dest[h, WIN_LON * r : WIN_LON * (r + 1), :] = moved[:WIN_LON, :WIN]
            return carry

        lax.fori_loop(0, src.shape[0], one_head, 0)


def table_strips(table):
    entry = jnp.arange(SPAN_LAT * SPAN_LON)[:, None, None]
    lon_i = jnp.arange(WIN_LON)[None, :, None]
    lane = jnp.arange(BAND)[None, None, :]
    wanted = (SPAN_LAT - 1 - lane // WIN_LON) * SPAN_LON + lon_i - lane % WIN_LON + WIN_LON - 1
    onehot = ((entry == wanted) & (lane < SPAN_LAT * WIN_LON)).astype(jnp.float32)
    strips = jnp.dot(table, onehot.reshape(entry.shape[0], -1), precision=lax.Precision.HIGHEST)
    return strips.reshape(table.shape[0], WIN_LON, BAND)


def all_bias(*tables):
    strips = [table_strips(table) for table in tables]
    return pl.pallas_call(
        bias_kernel,
        out_shape=[jax.ShapeDtypeStruct((t.shape[0], WIN, WIN), jnp.float32) for t in tables],
        in_specs=[VMEM] * len(tables),
        out_specs=[VMEM] * len(tables),
        compiler_params=PARAMS,
    )(*strips)


def across(first, second, one, two):
    def send(array):
        firsts, seconds = lax.axis_size(first), lax.axis_size(second)
        pairs = [
            (i * seconds + j, (i + one) % firsts * seconds + (j + two) % seconds)
            for i in range(firsts)
            for j in range(seconds)
        ]
        return lax.ppermute(array, (first, second), pairs)

    return send


def along(axis, step):
    return lambda array: lax.ppermute(array, axis, shifts(lax.axis_size(axis), step))


def forward(grid):
    right = along("lon", -1)(grid[HALF_LAT:, :HALF_LON])
    below = along("lat", -1)(grid[:HALF_LAT, HALF_LON:])
    corner = across("lon", "lat", -1, -1)(grid[:HALF_LAT, :HALF_LON])
    upper = jnp.concatenate([grid[HALF_LAT:, HALF_LON:], right], axis=1)
    lower = jnp.concatenate([below, corner], axis=1)
    return jnp.concatenate([upper, lower], axis=0)


def backward(grid):
    left = along("lon", 1)(grid[:-HALF_LAT, -HALF_LON:])
    above = along("lat", 1)(grid[-HALF_LAT:, :-HALF_LON])
    corner = across("lon", "lat", 1, 1)(grid[-HALF_LAT:, -HALF_LON:])
    upper = jnp.concatenate([corner, above], axis=1)
    lower = jnp.concatenate([left, grid[:-HALF_LAT, :-HALF_LON]], axis=1)
    return jnp.concatenate([upper, lower], axis=0)


def split_windows(grid):
    lats, lons = grid.shape[:2]
    blocked = grid.reshape((lats // WIN_LAT, WIN_LAT, lons // WIN_LON, WIN_LON) + grid.shape[2:])
    return jnp.moveaxis(blocked, 2, 1).reshape((-1, WIN) + grid.shape[2:])


def join_windows(windows, lats, lons):
    blocked = windows.reshape(
        (lats // WIN_LAT, lons // WIN_LON, WIN_LAT, WIN_LON) + windows.shape[2:]
    )
    return jnp.moveaxis(blocked, 2, 1).reshape((lats, lons) + windows.shape[2:])


def group_patches(grid):
    lats, lons, features = grid.shape
    blocked = grid.reshape(lats // 2, 2, lons // 2, 2, features)
    return jnp.moveaxis(blocked, 2, 1).reshape(-1, 4 * features)


def with_tags(tokens, fine_tags, coarse_tags):
    spread = jnp.repeat(jnp.repeat(coarse_tags, 2, axis=0), 2, axis=1)
    lane = jnp.arange(LANES)
    extra = jnp.where(
        lane == FINE_TAG,
        fine_tags[:, :, None],
        jnp.where(lane == COARSE_TAG, spread[:, :, None], 0),
    )
    return jnp.concatenate([tokens, extra.astype(tokens.dtype)], axis=-1)


def shards(
    tokens,
    fine_tags,
    coarse_tags,
    fine_gain,
    fine_inward,
    fine_outward,
    fine_table,
    merge_gain,
    merge_weight,
    coarse_gain,
    coarse_inward,
    coarse_outward,
    coarse_table,
):
    lats, lons, features = tokens.shape[1:]
    fine_weight = gather(jnp.concatenate([*fine_inward, fine_outward], axis=1))
    between_weight = gather(merge_weight)
    coarse_weight = gather(jnp.concatenate([*coarse_inward, coarse_outward], axis=1))
    fine_bias, coarse_bias = all_bias(fine_table, coarse_table)
    tagged = with_tags(tokens[0], fine_tags[0], coarse_tags[0])
    stream = split_windows(forward(tagged))
    fine = window_block(
        stream, lons // WIN_LON, features, FINE_TAG, fine_gain, fine_weight, fine_bias
    )
    fine_grid = join_windows(fine, lats, lons)
    grouped = group_patches(forward(fine_grid))
    coarse_in = merge(split_windows(grouped.reshape(lats // 2, lons // 2, -1)).reshape(grouped.shape),
                      features, merge_gain, between_weight)
    coarse = window_block(
        coarse_in.reshape((-1, WIN) + coarse_in.shape[1:]),
        lons // 2 // WIN_LON,
        2 * features,
        COARSE_TAG,
        coarse_gain,
        coarse_weight,
        coarse_bias,
    )
    coarse_grid = join_windows(coarse[:, :, : 2 * features], lats // 2, lons // 2)
    return backward(fine_grid[:, :, :features])[None], backward(coarse_grid)[None]


def solution(mesh):
    placed = (
        P(("grp", "lvl"), "lat", "lon", None),
        P(("grp", "lvl"), "lat", "lon"),
        P(("grp", "lvl"), "lat", "lon"),
        P(),
        P(None, "lon", "lvl"),
        P("lon", "lvl"),
        P(),
        P(),
        P("lon", "lvl"),
        P(),
        P(None, "lon", "lvl"),
        P("lon", "lvl"),
        P(),
    )
    return jax.shard_map(
        shards,
        mesh=mesh,
        in_specs=placed,
        out_specs=(P(("grp", "lvl"), "lat", "lon", None), P(("grp", "lvl"), "lat", "lon", None)),
        check_vma=False,
    )
```
